32 devices in a mesh: seq: 8 (over z, x), tp: 4 (over y, core).
Axes of the slice: x: 2, y: 2, z: 4, core: 2. Of those that a mesh axis runs over, the one named last changes fastest.
Arguments:
- mixer_input: bfloat16 [2048, 16384], P('seq', 'tp'), may hold values from -512 to 512
- mixer_gate: bfloat16 [2048, 16384], P('seq', 'tp'), may hold values from -5 to 5
- state_write: bfloat16 [2048, 128], P('seq'), may hold values from -6 to 6
- state_read: bfloat16 [2048, 128], P('seq'), may hold values from -0.5 to 0.5
- log_decay: float32 [128, 2048], P('tp', 'seq'), may hold values from -1 to 0
- norm_gain: float32 [16384], P('tp'), may hold values from 0.1 to 1.9
- queries: bfloat16 [2048, 8192], P('seq', 'tp'), may hold values from -25 to 25
- key_matrix_rows: bfloat16 [2048, 1024], P('seq', 'tp'), may hold values from -25 to 25
- value_matrix_rows: bfloat16 [2048, 1024], P('seq', 'tp'), may hold values from -6 to 6
- request_blocks: int32 [4], replicated, may hold values from 1 to 8, as said below
Outputs:
- mixer_out: bfloat16 [2048, 16384], P('seq', 'tp')
- attention_out: bfloat16 [2048, 8192], P('seq', 'tp')
The draws below stay inside these ranges and needn't reach their ends.
Inputs may be any that keep to these rules, and one draw needn't show every extreme that they name: `request_blocks`: requests are packed in order and fill the sequence; the second request holds exactly 8 blocks.
All inputs are finite; a program needn't handle non-finite values.
Results may differ from the reference program's by a relative error of at most 0.011.
Values may be sent and summed in bfloat16 or wider, within the bound.
A program may use at most 128 MiB of HBM per device.

```python
import math
import jax
import jax.numpy as jnp
from jax import lax

HEADS = 128
P_SIZE = 128
N = 128
QUERY_HEAD_COUNT = 64
KEY_VALUE_HEADS = 8
HEAD_WIDTH = 128
SEGMENT_SIZE = 256
CYCLE = 4
MOST_SLABS = 4
JOINED_SIZE = 2048
BLOCKS = 16
MOST_BLOCKS = 8
N_SEQ = 8


def attention_pair(key):
    random_query_draw = jnp.clip(jax.random.normal(jax.random.fold_in(key, 101), (JOINED_SIZE, QUERY_HEAD_COUNT * HEAD_WIDTH), jnp.float32), -5.0, 5.0)
    random_key_draw = jnp.clip(jax.random.normal(jax.random.fold_in(key, 102), (JOINED_SIZE, KEY_VALUE_HEADS * HEAD_WIDTH), jnp.float32), -5.0, 5.0)
    return (random_query_draw, random_key_draw)


def draw_queries(key, part):
    return attention_pair(key)[0].astype(jnp.bfloat16)


def draw_key_matrix_rows(key, part):
    return attention_pair(key)[1].astype(jnp.bfloat16)


def draw_request_blocks(key, part):
    remaining = BLOCKS - MOST_BLOCKS
    first_len = jax.random.randint(jax.random.fold_in(key, 401), (), 1, remaining - 1)
    third_len = jax.random.randint(jax.random.fold_in(key, 402), (), 1, remaining - first_len)
    fourth_len = remaining - first_len - third_len
    return jnp.stack([first_len, jnp.asarray(MOST_BLOCKS, jnp.int32), third_len, fourth_len]).astype(jnp.int32)


def draw_mixer_input(key, part):
    noise = jnp.clip(jax.random.normal(jax.random.fold_in(key, 201), (JOINED_SIZE, HEADS, P_SIZE), jnp.float32), -4.0, 4.0)
    ramp_top = 4.0
    head_scale = ramp_top ** (jnp.arange(HEADS, dtype=jnp.float32) / (HEADS - 1))
    channel_scale = jnp.exp(jax.random.uniform(jax.random.fold_in(key, 202), (HEADS, P_SIZE), jnp.float32, 0.0, math.log(2.5)))
    row_scale = jnp.exp(jax.random.uniform(jax.random.fold_in(key, 203), (JOINED_SIZE,), jnp.float32, math.log(1.0 / 3.0), math.log(10.0 / 3.0)))
    payload_array = noise * head_scale[None, :, None] * channel_scale[None] * row_scale[:, None, None]
    return payload_array.reshape(JOINED_SIZE, HEADS * P_SIZE).astype(jnp.bfloat16)


def draw_log_decay(key, part):
    chain_tokens = MOST_SLABS * SEGMENT_SIZE
    fast_cut = 4
    is_fast = jax.random.randint(jax.random.fold_in(key, 301), (HEADS,), 0, 8) < fast_cut
    fast_rate = 1.0 / jax.random.uniform(jax.random.fold_in(key, 302), (HEADS,), jnp.float32, 30.0, 50.0)
    slow_rate = jnp.exp(jax.random.uniform(jax.random.fold_in(key, 303), (HEADS,), jnp.float32, math.log(0.02), math.log(0.2))) / chain_tokens
    fading_speed = jnp.where(is_fast, fast_rate, slow_rate)
    slab_factor = jnp.exp(jax.random.uniform(jax.random.fold_in(key, 304), (HEADS, N_SEQ), jnp.float32, math.log(0.5), math.log(2.0)))
    slice_lines = jnp.repeat(slab_factor, SEGMENT_SIZE, axis=1)
    approximate_guess = jax.random.uniform(jax.random.fold_in(key, 305), (HEADS, JOINED_SIZE), jnp.float32, 0.5, 1.5)
    run_extent = jax.random.randint(jax.random.fold_in(key, 306), (JOINED_SIZE,), 0, 4 * SEGMENT_SIZE) == 0
    stack_level = jax.random.uniform(jax.random.fold_in(key, 307), (JOINED_SIZE,), jnp.float32, 0.5, 0.8)
    payload_array = -fading_speed[:, None] * slice_lines * approximate_guess + jnp.where(run_extent, jnp.log(stack_level), 0.0)[None, :]
    return payload_array.astype(jnp.float32)


def block_scale(stream_key, shape, cuts, least, high):
    def one(position, blocks):
        heights = jax.random.uniform(jax.random.fold_in(jax.random.fold_in(stream_key, 6), position), (blocks,), jnp.float32, least / len(cuts), high / len(cuts))
        return jnp.repeat(jnp.exp(heights), shape[position] // blocks).reshape((-1,) + (1,) * (len(shape) - position - 1))

    gain = one(*cuts[0])
    for cut in cuts[1:]:
        gain = gain * one(*cut)
    return gain


def centred(stream_key, extent, deviation, limit, shards=(), held_as=jnp.bfloat16):
    factor_of = block_scale(stream_key, extent, shards, -0.22, 0.18) if shards else 1.0
    array = jax.random.normal(stream_key, extent, jnp.float32) * deviation * factor_of
    return jnp.minimum(jnp.maximum(array, -limit), limit).astype(held_as)


def setup_inputs(seed: int = 0) -> dict:
    splits = jax.random.split(jax.random.key(seed), 11)
    return {
        "mixer_input": draw_mixer_input(jax.random.fold_in(splits[10], 71), 0),
        "mixer_gate": centred(splits[1], (JOINED_SIZE, HEADS * P_SIZE), 1.0, 5.0, ((0, 8), (1, 4))),
        "state_write": centred(splits[2], (JOINED_SIZE, N), 1.0, 6.0, ((0, 8),)),
        "state_read": centred(splits[3], (JOINED_SIZE, N), 0.09, 0.5, ((0, 8),)),
        "log_decay": draw_log_decay(jax.random.fold_in(splits[10], 71), 0),
        "norm_gain": jnp.clip(1.0 + 0.18 * jax.random.normal(splits[5], (HEADS * P_SIZE,), jnp.float32), 0.1, 1.9),
        "queries": draw_queries(jax.random.fold_in(splits[10], 71), 0),
        "key_matrix_rows": draw_key_matrix_rows(jax.random.fold_in(splits[10], 71), 0),
        "value_matrix_rows": centred(splits[8], (JOINED_SIZE, KEY_VALUE_HEADS * HEAD_WIDTH), 1.0, 6.0, ((0, 8), (1, 4))),
        "request_blocks": draw_request_blocks(jax.random.fold_in(splits[10], 71), 0),
    }


def segment_ids(request_blocks, positions):
    request_ends = jnp.cumsum(request_blocks).astype(jnp.int32) * 128
    counted = lax.optimization_barrier(jnp.sum((positions[:, None] >= request_ends[None, :]).astype(jnp.int32), axis=1))
    return jnp.where(positions < 0, -1, counted).astype(jnp.int32)

def mixer_part(mixer_input, mixer_gate, state_write, state_read, log_decay, norm_gain, segment):
    block_count = JOINED_SIZE // 128
    inputs = mixer_input.reshape(block_count, 128, HEADS, P_SIZE)
    gates = mixer_gate.reshape(block_count, 128, HEADS, P_SIZE)
    writes = state_write.reshape(block_count, 128, N)
    read_rows = state_read.reshape(block_count, 128, N)
    decays = log_decay.reshape(HEADS, block_count, 128).transpose(1, 0, 2)
    labels = segment.reshape(block_count, 128)
    before = jnp.concatenate([jnp.full((1,), -1, jnp.int32), labels[:-1, -1]]).astype(jnp.int32)
    causal = jnp.tril(jnp.ones((128, 128), dtype=bool))

    def advance(running_state, item):
        block_inputs, block_gates, block_writes, block_reads, block_decays, block_labels, label_before = item
        running = jnp.cumsum(block_decays, axis=1)
        shared = ((block_labels[:, None] == block_labels[None, :]) & causal)[None]
        spread = jnp.where(shared, running[:, :, None] - running[:, None, :], 0.0)
        weight = jnp.where(shared, jnp.exp(spread), 0.0)
        affinity = jnp.dot(block_reads, block_writes.T, preferred_element_type=jnp.float32)
        mixing = lax.optimization_barrier((weight * affinity[None]).astype(jnp.bfloat16))
        within = jnp.einsum('hij,jhp->ihp', mixing.astype(jnp.float32), block_inputs.astype(jnp.float32))
        opened = block_labels == label_before
        entry_decay = jnp.where(opened[None, :], jnp.exp(running), 0.0)
        from_state = jnp.einsum('in,hnp->ihp', block_reads.astype(jnp.float32), running_state, precision=lax.Precision.HIGHEST)
        mixed = within + from_state * entry_decay.T[:, :, None]
        gated = mixed * jax.nn.silu(block_gates.astype(jnp.float32))
        mean_square = lax.optimization_barrier(jnp.mean(gated * gated, axis=(1, 2)))
        scaling = lax.rsqrt(mean_square + 1e-05)
        block_out = ((gated * scaling[:, None, None]).reshape(128, HEADS * P_SIZE) * norm_gain[None, :]).astype(jnp.bfloat16)
        reaching = jnp.where((block_labels == block_labels[-1])[None, :], jnp.exp(running[:, -1:] - running), 0.0)
        carried = lax.optimization_barrier((block_inputs.astype(jnp.float32) * reaching.T[:, :, None]).astype(jnp.bfloat16))
        block_state = jnp.einsum('jn,jhp->hnp', block_writes.astype(jnp.float32), carried.astype(jnp.float32))
        block_decay = jnp.where(opened[-1], jnp.exp(running[:, -1]), 0.0)
        return (block_decay[:, None, None] * running_state + block_state, block_out)
    start_state = jnp.zeros((HEADS, N, P_SIZE), jnp.float32)
    final_state, outputs = lax.scan(advance, start_state, (inputs, gates, writes, read_rows, decays, labels, before))
    return outputs.reshape(JOINED_SIZE, HEADS * P_SIZE)

def attention_part(queries, key_matrix_rows, value_matrix_rows, segment):
    query_group = QUERY_HEAD_COUNT // KEY_VALUE_HEADS
    token_span = (CYCLE + 1) * SEGMENT_SIZE
    error_margin = CYCLE * SEGMENT_SIZE
    scale = 1.0 / math.sqrt(HEAD_WIDTH)
    keys_with_padding = jnp.concatenate([jnp.zeros((error_margin, KEY_VALUE_HEADS * HEAD_WIDTH), jnp.bfloat16), key_matrix_rows])
    values_with_padding = jnp.concatenate([jnp.zeros((error_margin, KEY_VALUE_HEADS * HEAD_WIDTH), jnp.bfloat16), value_matrix_rows])
    padded_segment = jnp.concatenate([jnp.full((error_margin,), -1, jnp.int32), segment]).astype(jnp.int32)
    padded_positions = (jnp.arange(JOINED_SIZE + error_margin) - error_margin).astype(jnp.int32)

    def slab_fn(slab):
        first_entry = (slab * SEGMENT_SIZE).astype(jnp.int32)
        block_of_queries = lax.dynamic_slice_in_dim(queries, first_entry, SEGMENT_SIZE, 0).reshape(SEGMENT_SIZE, KEY_VALUE_HEADS, query_group, HEAD_WIDTH)
        block_of_keys = lax.dynamic_slice_in_dim(keys_with_padding, first_entry, token_span, 0).reshape(token_span, KEY_VALUE_HEADS, HEAD_WIDTH)
        block_of_values = lax.dynamic_slice_in_dim(values_with_padding, first_entry, token_span, 0).reshape(token_span, KEY_VALUE_HEADS, HEAD_WIDTH)
        query_segment = lax.dynamic_slice_in_dim(segment, first_entry, SEGMENT_SIZE, 0)
        query_positions = (first_entry + jnp.arange(SEGMENT_SIZE)).astype(jnp.int32)
        key_segment = lax.dynamic_slice_in_dim(padded_segment, first_entry, token_span, 0)
        key_positions = lax.dynamic_slice_in_dim(padded_positions, first_entry, token_span, 0)
        allowed = (query_segment[:, None] == key_segment[None, :]) & (key_positions[None, :] <= query_positions[:, None])

        def per_head_attend(head):
            query_head = block_of_queries[:, head].astype(jnp.float32)
            key_head = block_of_keys[:, head].astype(jnp.float32)
            value_head = block_of_values[:, head].astype(jnp.float32)
            scores = jnp.einsum('tgd,sd->gts', query_head, key_head) * scale
            masked = jnp.where(allowed[None], scores, -jnp.inf)
            largest = lax.optimization_barrier(jnp.max(masked, axis=2, keepdims=True))
            weights = jnp.where(allowed[None], jnp.exp(masked - largest), 0.0)
            totals = lax.optimization_barrier(jnp.sum(weights, axis=2))
            rounded = lax.optimization_barrier(weights.astype(jnp.bfloat16))
            summed = jnp.einsum('gts,sd->tgd', rounded.astype(jnp.float32), value_head)
            return summed / totals.T[:, :, None]
        output_per_head = lax.map(per_head_attend, jnp.arange(KEY_VALUE_HEADS).astype(jnp.int32))
        return output_per_head.transpose(1, 0, 2, 3).reshape(SEGMENT_SIZE, QUERY_HEAD_COUNT * HEAD_WIDTH).astype(jnp.bfloat16)
    slabs = lax.map(slab_fn, jnp.arange(N_SEQ).astype(jnp.int32))
    return slabs.reshape(JOINED_SIZE, QUERY_HEAD_COUNT * HEAD_WIDTH)

def reference(mixer_input, mixer_gate, state_write, state_read, log_decay, norm_gain, queries, key_matrix_rows, value_matrix_rows, request_blocks):
    positions = jnp.arange(JOINED_SIZE).astype(jnp.int32)
    segment = segment_ids(request_blocks, positions)
    mixer_out = mixer_part(mixer_input, mixer_gate, state_write, state_read, log_decay, norm_gain, segment)
    attention_out = attention_part(queries, key_matrix_rows, value_matrix_rows, segment)
    return (mixer_out, attention_out)
```

```python
from functools import partial
import math

import jax
import jax.numpy as jnp
from jax import lax
from jax.experimental import pallas as pl
from jax.experimental.pallas import tpu as pltpu
from jax.sharding import PartitionSpec as P

WIDTH = 128
BLOCK = 128
CYCLE = 4
CHUNK = 4
FAR = -1e30
MESH = pl.DeviceIdType.MESH
HIGH = lax.Precision.HIGHEST


def lanes(h):
    return pl.ds(pl.multiple_of(h * WIDTH, WIDTH), WIDTH)


def dot_t(a, b, precision=None):
    return lax.dot_general(
        a, b, (((1,), (1,)), ((), ())), preferred_element_type=jnp.float32, precision=precision
    )


def dot(a, b, precision=None):
    return jnp.dot(a, b, preferred_element_type=jnp.float32, precision=precision)


def kernel(
    n_seq, n_tp, features,
    rb, x_ref, g_ref, b_ref, c_ref, ld_ref, gain_ref, q_ref, k_ref, v_ref,
    out_ref, att_ref,
    kv, bias, run, colb, bt, aff, wbuf, s0, slab, partner_s, ent, ent_own, eout,
    gdec, gpart, sq, ss, ssbuf,
    kv_send, kv_recv, st_send, st_recv, ev_send, e_recv, ch_send, gd_sem, ss_send, ss_recv,
):
    d = lax.axis_index("seq")
    t = lax.axis_index("tp")
    odd = lax.rem(d, 2)
    is_odd = odd == 1
    is_even = odd == 0
    partner = d + 1 - 2 * odd
    has_next = d + 2 < n_seq
    has_prev = d >= 2
    rows = x_ref.shape[0]
    heads = ld_ref.shape[0]
    q_heads = q_ref.shape[1] // WIDTH
    kv_heads = k_ref.shape[1] // WIDTH
    group = q_heads // kv_heads
    chunks = heads // CHUNK
    half = (slice(0, BLOCK), slice(BLOCK, 2 * BLOCK))

    barrier = pltpu.get_barrier_semaphore()
    pl.semaphore_signal(barrier, inc=1, device_id={"seq": partner}, device_id_type=MESH)
    for r in range(1, n_tp):
        pl.semaphore_signal(
            barrier, inc=1, device_id={"tp": lax.rem(t + r, n_tp)}, device_id_type=MESH
        )

    @pl.when(has_next)
    def _():
        pl.semaphore_signal(barrier, inc=1, device_id={"seq": d + 2}, device_id_type=MESH)

    @pl.when(has_prev)
    def _():
        pl.semaphore_signal(barrier, inc=1, device_id={"seq": d - 2}, device_id_type=MESH)

    peers = n_tp + has_next.astype(jnp.int32) + has_prev.astype(jnp.int32)
    pl.semaphore_wait(barrier, peers)

    def kv_copy(part, source, send, slot, target):
        own = (k_ref, v_ref)[part]
        return pltpu.make_async_remote_copy(
            src_ref=own if source is None else kv.at[source, part],
            dst_ref=kv.at[slot, part],
            send_sem=kv_send.at[send, part],
            recv_sem=kv_recv.at[slot, part],
            device_id={"seq": target},
            device_id_type=MESH,
        )

    own_up = (has_next, None, 0, 1, d + 2)
    own_side = (is_even, None, 1, 0, d + 1)
    relay_up = (has_prev & has_next, 1, 2, 3, d + 2)
    relay_even = (has_prev & is_even, 1, 1 + 2, 2, d + 1)
    relay_odd = (has_prev & is_odd, 1, 1 + 2, 0, d - 1)
    last_odd = ((d >= 4) & is_odd, 3, 4, 2, d - 1)

    def start(move):
        @pl.when(move[0])
        def _():
            for part in range(2):
                kv_copy(part, *move[1:]).start()

    def sent(move):
        @pl.when(move[0])
        def _():
            for part in range(2):
                kv_copy(part, *move[1:]).wait_send()

    def arrived(slot):
        @pl.when(d >= slot + 1)
        def _():
            for part in range(2):
                kv_copy(part, None, 0, slot, partner).wait_recv()

    start(own_up)
    start(own_side)
    for slot in range(CYCLE):
        @pl.when(d < slot + 1)
        def _():
            kv[slot] = jnp.zeros(kv.shape[1:], kv.dtype)

    @pl.when(d < 2)
    def _():
        ent[...] = jnp.zeros(ent.shape, ent.dtype)

    ends = []
    total = jnp.int32(0)
    for i in range(4):
        total = total + rb[i]
        ends.append(total)

    def opened(block):
        flag = jnp.where(block == 0, 0.0, 1.0)
        for e in ends:
            flag = flag * jnp.where(block == e, 0.0, 1.0)
        return flag

    open_0 = opened(2 * d)
    open_1 = opened(2 * d + 1)
    opens = (open_0, open_1)

    i_r = lax.broadcasted_iota(jnp.int32, (rows, rows), 0)
    i_c = lax.broadcasted_iota(jnp.int32, (rows, rows), 1)
    lower = jnp.where((i_c <= i_r) & (i_r // BLOCK == i_c // BLOCK), 1.0, 0.0)
    decays = ld_ref[...]
    sums_row = dot_t(decays, lower, HIGH)
    columns = dot_t(lower, decays, HIGH)
    for h in range(heads):
        colb[h] = jnp.broadcast_to(columns[:, h : h + 1], (rows, WIDTH))
        run[h] = sums_row[h : h + 1, :]
        gdec[h] = open_0 * open_1 * jnp.exp(
            colb[h, BLOCK - 1 : BLOCK, :] + colb[h, 2 * BLOCK - 1 : 2 * BLOCK, :]
        )

    def decay_copy():
        return pltpu.make_async_remote_copy(
            src_ref=gdec, dst_ref=gpart, send_sem=gd_sem.at[0], recv_sem=gd_sem.at[1],
            device_id={"seq": partner}, device_id_type=MESH,
        )

    @pl.when(is_even)
    def _():
        decay_copy().start()

    bt[...] = b_ref[...].astype(jnp.float32).T.astype(jnp.bfloat16)

    def part_of(ref, c):
        return ref.at[pl.ds(c * CHUNK, CHUNK)]

    def slab_copy(c):
        return pltpu.make_async_remote_copy(
            src_ref=part_of(slab, c), dst_ref=part_of(partner_s, c),
            send_sem=st_send.at[c], recv_sem=st_recv.at[c],
            device_id={"seq": partner}, device_id_type=MESH,
        )

    def side_copy(c):
        return pltpu.make_async_remote_copy(
            src_ref=part_of(ent, c), dst_ref=part_of(ent, c),
            send_sem=ev_send.at[c], recv_sem=e_recv.at[c],
            device_id={"seq": d - 1}, device_id_type=MESH,
        )

    def chain_copy(c):
        return pltpu.make_async_remote_copy(
            src_ref=part_of(eout, c), dst_ref=part_of(ent, c),
            send_sem=ch_send.at[c], recv_sem=e_recv.at[c],
            device_id={"seq": d + 2}, device_id_type=MESH,
        )

    def state_of(h):
        states = []
        for b in range(2):
            last_row = colb[h, b * BLOCK + BLOCK - 1 : b * BLOCK + BLOCK, :]
            reach = jnp.exp(last_row - colb[h, half[b], :])
            carried = (x_ref[half[b], lanes(h)].astype(jnp.float32) * reach).astype(jnp.bfloat16)
            states.append(dot(bt[:, half[b]], carried))
        g_1 = open_1 * jnp.exp(colb[h, 2 * BLOCK - 1 : 2 * BLOCK, :])
        s0[h] = states[0].astype(jnp.bfloat16)
        slab[h] = (g_1 * states[0] + states[1]).astype(jnp.bfloat16)

    def state_chunk(c, carry):
        for i in range(CHUNK):
            state_of(c * CHUNK + i)

        @pl.when(is_even)
        def _():
            slab_copy(c).start()

        return carry

    lax.fori_loop(0, chunks, state_chunk, 0)

    arrived(1)
    start(relay_up)
    start(relay_even)
    start(relay_odd)

    for b in range(2):
        aff[b] = dot_t(c_ref[half[b], :], b_ref[half[b], :])
    causal = lax.broadcasted_iota(jnp.int32, (BLOCK, BLOCK), 1) <= lax.broadcasted_iota(
        jnp.int32, (BLOCK, BLOCK), 0
    )

    def within_of(h, carry):
        for b in range(2):
            spread = colb[h, half[b], :] - run[h, :, half[b]]
            weight = jnp.exp(jnp.where(causal, spread, FAR))
            mixing = (weight * aff[b]).astype(jnp.bfloat16)
            wbuf[half[b], lanes(h)] = dot(mixing, x_ref[half[b], lanes(h)])
        return carry

    lax.fori_loop(0, heads, within_of, 0)

    def label(positions):
        found = jnp.zeros(positions.shape, jnp.int32)
        for e in ends:
            found = found + jnp.where(positions >= e * BLOCK, 1, 0)
        return jnp.where(positions < 0, -1, found)

    q_pos = d * rows + lax.broadcasted_iota(jnp.int32, (rows, 1), 0)
    q_label = label(q_pos)
    for slot in range(CYCLE + 1):
        k_pos = (d - slot) * rows + lax.broadcasted_iota(jnp.int32, (1, rows), 1)
        same = (q_label == label(k_pos)) & (k_pos <= q_pos)
        bias[slot] = jnp.where(same, 0.0, FAR)

    arrived(3)
    start(last_odd)
    arrived(0)
    arrived(2)

    @pl.when(is_odd)
    def _():
        decay_copy().wait_recv()

    factor = math.log2(math.e) / math.sqrt(WIDTH)

    def attend(h):
        kh = h // group
        query = q_ref[:, lanes(h)]
        scores = []
        for slot in range(CYCLE + 1):
            key = k_ref[:, lanes(kh)] if slot == 0 else kv[slot - 1, 0, :, lanes(kh)]
            scores.append(dot_t(query, key) + bias[slot])
        top = scores[0]
        for s in scores[1:]:
            top = jnp.maximum(top, s)
        top = jnp.max(top, axis=1, keepdims=True)
        sums = jnp.zeros((rows, rows), jnp.float32)
        result = jnp.zeros((rows, WIDTH), jnp.float32)
        for slot in range(CYCLE + 1):
            value = v_ref[:, lanes(kh)] if slot == 0 else kv[slot - 1, 1, :, lanes(kh)]
            weight = jnp.exp2((scores[slot] - top) * factor)
            sums = sums + weight
            result = result + dot(weight.astype(jnp.bfloat16), value)
        result = result / jnp.sum(sums, axis=1, keepdims=True)
        att_ref[:, lanes(h)] = result.astype(jnp.bfloat16)

    def relay(c):
        slab_copy(c).wait_recv()

        @pl.when(has_prev)
        def _():
            chain_copy(c).wait_recv()
            side_copy(c).start()

        for i in range(CHUNK):
            h = c * CHUNK + i
            own = gpart[h] * ent[h].astype(jnp.float32) + partner_s[h].astype(
                jnp.float32
            )
            ent_own[h] = own.astype(jnp.bfloat16)
            after = gdec[h] * own + slab[h].astype(jnp.float32)
            eout[h] = after.astype(jnp.bfloat16)

        @pl.when(has_next)
        def _():
            chain_copy(c).start()

    per = q_heads // chunks

    def both(c, carry):
        for i in range(per):
            attend(c * per + i)

        @pl.when(is_odd)
        def _():
            relay(c)

        return carry

    lax.fori_loop(0, chunks, both, 0)

    sq[...] = jnp.zeros(sq.shape, jnp.float32)

    def finish_of(h):
        entering = ent_own[h].astype(jnp.float32)
        g_0 = open_0 * jnp.exp(colb[h, BLOCK - 1 : BLOCK, :])
        later = g_0 * entering + s0[h].astype(jnp.float32)
        states = (ent_own[h], later.astype(jnp.bfloat16))
        for b in range(2):
            from_state = dot(c_ref[half[b], :], states[b])
            entry = opens[b] * jnp.exp(colb[h, half[b], :])
            mixed = wbuf[half[b], lanes(h)] + from_state * entry
            gate = g_ref[half[b], lanes(h)].astype(jnp.float32)
            gated = mixed * (gate / (1.0 + jnp.exp(-gate)))
            wbuf[half[b], lanes(h)] = gated
            sq[half[b], :] = sq[half[b], :] + gated * gated

    def finish(c, carry):
        @pl.when(is_even)
        def _():
            @pl.when(has_prev)
            def _():
                side_copy(c).wait_recv()

            ent_own[pl.ds(c * CHUNK, CHUNK)] = ent[pl.ds(c * CHUNK, CHUNK)]

        for i in range(CHUNK):
            finish_of(c * CHUNK + i)
        return carry

    lax.fori_loop(0, chunks, finish, 0)

    ss[...] = dot_t(jnp.ones((8, WIDTH), jnp.float32), sq[...], HIGH)

    def squares_copy(r):
        return pltpu.make_async_remote_copy(
            src_ref=ss, dst_ref=ssbuf.at[r - 1], send_sem=ss_send.at[r - 1],
            recv_sem=ss_recv.at[r - 1], device_id={"tp": lax.rem(t + r, n_tp)},
            device_id_type=MESH,
        )

    for r in range(1, n_tp):
        squares_copy(r).start()
    squares = ss[...]
    for r in range(1, n_tp):
        squares_copy(r).wait_recv()
        squares = squares + ssbuf[r - 1]
    spread_out = lax.dot_general(
        squares, jnp.full((8, WIDTH), 0.125, jnp.float32), (((0,), (0,)), ((), ())),
        preferred_element_type=jnp.float32, precision=HIGH,
    )
    sq[...] = lax.rsqrt(spread_out / features + 1e-05)

    def scale_out(h, carry):
        out_ref[:, lanes(h)] = (
            wbuf[:, lanes(h)] * sq[...] * gain_ref[:, lanes(h)]
        ).astype(jnp.bfloat16)
        return carry

    lax.fori_loop(0, heads, scale_out, 0)

    for r in range(1, n_tp):
        squares_copy(r).wait_send()
    for move in (own_up, own_side, relay_up, relay_even, relay_odd, last_odd):
        sent(move)

    @pl.when(is_even)
    def _():
        decay_copy().wait_send()

    def drain(c, carry):
        @pl.when(is_even)
        def _():
            slab_copy(c).wait_send()

        @pl.when(is_odd & has_prev)
        def _():
            side_copy(c).wait_send()

        @pl.when(is_odd & has_next)
        def _():
            chain_copy(c).wait_send()

        return carry

    lax.fori_loop(0, chunks, drain, 0)


def on_device(n_seq, n_tp, *args):
    (x, gate, write, read, decay, gain, q, k, v, request_blocks) = args
    rows = x.shape[0]
    heads = decay.shape[0]
    chunks = heads // CHUNK
    f32, bf16 = jnp.float32, jnp.bfloat16
    states = pltpu.VMEM((heads, WIDTH, WIDTH), bf16)
    dma = pltpu.SemaphoreType.DMA
    vmem = pl.BlockSpec(memory_space=pltpu.VMEM)
    return pl.pallas_call(
        partial(kernel, n_seq, n_tp, heads * n_tp * WIDTH),
        out_shape=(
            jax.ShapeDtypeStruct(x.shape, bf16),
            jax.ShapeDtypeStruct(q.shape, bf16),
        ),
        in_specs=[pl.BlockSpec(memory_space=pltpu.SMEM)] + [vmem] * 9,
        out_specs=(vmem, vmem),
        scratch_shapes=[
            pltpu.VMEM((CYCLE, 2) + k.shape, bf16),
            pltpu.VMEM((CYCLE + 1, rows, rows), f32),
            pltpu.VMEM((heads, 1, rows), f32),
            pltpu.VMEM((heads, rows, WIDTH), f32),
            pltpu.VMEM((WIDTH, rows), bf16),
            pltpu.VMEM((2, BLOCK, BLOCK), f32),
            pltpu.VMEM(x.shape, f32),
            states, states, states, states, states, states,
            pltpu.VMEM((heads, 1, WIDTH), f32),
            pltpu.VMEM((heads, 1, WIDTH), f32),
            pltpu.VMEM((rows, WIDTH), f32),
            pltpu.VMEM((8, rows), f32),
            pltpu.VMEM((n_tp - 1, 8, rows), f32),
            dma((5, 2)), dma((CYCLE, 2)),
            dma((chunks,)), dma((chunks,)), dma((chunks,)), dma((chunks,)), dma((chunks,)),
            dma((2,)), dma((n_tp - 1,)), dma((n_tp - 1,)),
        ],
        compiler_params=pltpu.CompilerParams(
            collective_id=0, has_side_effects=True, vmem_limit_bytes=60 * 1024 * 1024
        ),
    )(request_blocks, x, gate, write, read, decay, gain.reshape(1, -1), q, k, v)


def solution(mesh):
    placed = (
        P("seq", "tp"),
        P("seq", "tp"),
        P("seq", None),
        P("seq", None),
        P("tp", "seq"),
        P("tp"),
        P("seq", "tp"),
        P("seq", "tp"),
        P("seq", "tp"),
        P(),
    )
    return jax.shard_map(
        partial(on_device, mesh.shape["seq"], mesh.shape["tp"]),
        mesh=mesh,
        in_specs=placed,
        out_specs=(P("seq", "tp"), P("seq", "tp")),
        check_vma=False,
    )
```

```python
from functools import partial
import math

import jax
import jax.numpy as jnp
from jax import lax
from jax.experimental import pallas as pl
from jax.experimental.pallas import tpu as pltpu
from jax.sharding import PartitionSpec as P

WIDTH = 128
BLOCK = 128
CYCLE = 4
CHUNK = 2
FAR = -1e30
MESH = pl.DeviceIdType.MESH
HIGH = lax.Precision.HIGHEST


def lanes(h):
    return pl.ds(pl.multiple_of(h * WIDTH, WIDTH), WIDTH)


def dot_t(a, b, precision=None):
    return lax.dot_general(
        a, b, (((1,), (1,)), ((), ())), preferred_element_type=jnp.float32, precision=precision
    )


def dot(a, b, precision=None):
    return jnp.dot(a, b, preferred_element_type=jnp.float32, precision=precision)


def kernel(
    n_seq, n_tp, features,
    rb, x_ref, g_ref, b_ref, c_ref, ld_ref, gain_ref, q_ref, k_ref, v_ref,
    out_ref, att_ref,
    kv, bias, run, colb, bt, aff, wbuf, s0, slab, partner_s, ent, ent_own, eout, eside,
    acc, tops, sums_of, gdec, gpart, sq, ss, ssbuf,
    kv_send, kv_recv, st_send, st_recv, ev_send, e_recv, ch_send, c_recv, gd_sem, ss_send, ss_recv,
):
    d = lax.axis_index("seq")
    t = lax.axis_index("tp")
    odd = lax.rem(d, 2)
    is_odd = odd == 1
    is_even = odd == 0
    partner = d + 1 - 2 * odd
    has_next = d + 2 < n_seq
    has_prev = d >= 2
    rows = x_ref.shape[0]
    heads = ld_ref.shape[0]
    q_heads = q_ref.shape[1] // WIDTH
    kv_heads = k_ref.shape[1] // WIDTH
    group = q_heads // kv_heads
    near = heads // CHUNK // 2
    mine = odd * near
    theirs = near - mine
    half = (slice(0, BLOCK), slice(BLOCK, 2 * BLOCK))

    barrier = pltpu.get_barrier_semaphore()
    pl.semaphore_signal(barrier, inc=1, device_id={"seq": partner}, device_id_type=MESH)
    for r in range(1, n_tp):
        pl.semaphore_signal(
            barrier, inc=1, device_id={"tp": lax.rem(t + r, n_tp)}, device_id_type=MESH
        )

    @pl.when(has_next)
    def _():
        pl.semaphore_signal(barrier, inc=1, device_id={"seq": d + 2}, device_id_type=MESH)

    @pl.when(has_prev)
    def _():
        pl.semaphore_signal(barrier, inc=1, device_id={"seq": d - 2}, device_id_type=MESH)

    peers = n_tp + has_next.astype(jnp.int32) + has_prev.astype(jnp.int32)
    pl.semaphore_wait(barrier, peers)

    def kv_copy(part, source, send, slot, target):
        own = (k_ref, v_ref)[part]
        return pltpu.make_async_remote_copy(
            src_ref=own if source is None else kv.at[source, part],
            dst_ref=kv.at[slot, part],
            send_sem=kv_send.at[send, part],
            recv_sem=kv_recv.at[slot, part],
            device_id={"seq": target},
            device_id_type=MESH,
        )

    own_up = (has_next, None, 0, 1, d + 2)
    own_side = (is_even, None, 1, 0, d + 1)
    relay_up = (has_prev & has_next, 1, 2, 3, d + 2)
    relay_even = (has_prev & is_even, 1, 1 + 2, 2, d + 1)
    relay_odd = (has_prev & is_odd, 1, 1 + 2, 0, d - 1)
    last_odd = ((d >= 4) & is_odd, 3, 4, 2, d - 1)

    def start(move):
        @pl.when(move[0])
        def _():
            for part in range(2):
                kv_copy(part, *move[1:]).start()

    def sent(move):
        @pl.when(move[0])
        def _():
            for part in range(2):
                kv_copy(part, *move[1:]).wait_send()

    def arrived(slot):
        @pl.when(d >= slot + 1)
        def _():
            for part in range(2):
                kv_copy(part, None, 0, slot, partner).wait_recv()

    start(own_up)
    start(own_side)
    for slot in range(CYCLE):
        @pl.when(d < slot + 1)
        def _():
            kv[slot] = jnp.zeros(kv.shape[1:], kv.dtype)

    span = near * CHUNK

    @pl.when(d < 2)
    def _():
        ent[pl.ds(mine * CHUNK, span)] = jnp.zeros((span,) + ent.shape[1:], ent.dtype)

    @pl.when((d < 2) & is_even)
    def _():
        ent_own[pl.ds(theirs * CHUNK, span)] = jnp.zeros((span,) + ent.shape[1:], ent.dtype)

    ends = []
    total = jnp.int32(0)
    for i in range(4):
        total = total + rb[i]
        ends.append(total)

    def opened(block):
        flag = jnp.where(block == 0, 0.0, 1.0)
        for e in ends:
            flag = flag * jnp.where(block == e, 0.0, 1.0)
        return flag

    open_0 = opened(2 * d)
    open_1 = opened(2 * d + 1)
    opens = (open_0, open_1)

    i_r = lax.broadcasted_iota(jnp.int32, (rows, rows), 0)
    i_c = lax.broadcasted_iota(jnp.int32, (rows, rows), 1)
    lower = jnp.where((i_c <= i_r) & (i_r // BLOCK == i_c // BLOCK), 1.0, 0.0)
    decays = ld_ref[...]
    sums_row = dot_t(decays, lower, HIGH)
    columns = dot_t(lower, decays, HIGH)
    for h in range(heads):
        colb[h] = jnp.broadcast_to(columns[:, h : h + 1], (rows, WIDTH))
        run[h] = sums_row[h : h + 1, :]
        gdec[h] = open_0 * open_1 * jnp.exp(
            colb[h, BLOCK - 1 : BLOCK, :] + colb[h, 2 * BLOCK - 1 : 2 * BLOCK, :]
        )

    def decay_copy():
        return pltpu.make_async_remote_copy(
            src_ref=gdec, dst_ref=gpart, send_sem=gd_sem.at[0], recv_sem=gd_sem.at[1],
            device_id={"seq": partner}, device_id_type=MESH,
        )

    decay_copy().start()
    bt[...] = b_ref[...].astype(jnp.float32).T.astype(jnp.bfloat16)

    def part_of(ref, c):
        return ref.at[pl.ds(c * CHUNK, CHUNK)]

    def slab_copy(c):
        return pltpu.make_async_remote_copy(
            src_ref=part_of(slab, c), dst_ref=part_of(partner_s, c),
            send_sem=st_send.at[c], recv_sem=st_recv.at[c],
            device_id={"seq": partner}, device_id_type=MESH,
        )

    def side_copy(c, source):
        return pltpu.make_async_remote_copy(
            src_ref=part_of(source, c), dst_ref=part_of(ent_own, c),
            send_sem=ev_send.at[c], recv_sem=e_recv.at[c],
            device_id={"seq": partner}, device_id_type=MESH,
        )

    def chain_copy(c):
        return pltpu.make_async_remote_copy(
            src_ref=part_of(eout, c), dst_ref=part_of(ent, c),
            send_sem=ch_send.at[c], recv_sem=c_recv.at[c],
            device_id={"seq": d + 2}, device_id_type=MESH,
        )

    def state_of(h):
        states = []
        for b in range(2):
            last_row = colb[h, b * BLOCK + BLOCK - 1 : b * BLOCK + BLOCK, :]
            reach = jnp.exp(last_row - colb[h, half[b], :])
            carried = (x_ref[half[b], lanes(h)].astype(jnp.float32) * reach).astype(jnp.bfloat16)
            states.append(dot(bt[:, half[b]], carried))
        g_1 = open_1 * jnp.exp(colb[h, 2 * BLOCK - 1 : 2 * BLOCK, :])
        s0[h] = states[0].astype(jnp.bfloat16)
        slab[h] = (g_1 * states[0] + states[1]).astype(jnp.bfloat16)

    def state_sent(i, carry):
        c = theirs + i
        for j in range(CHUNK):
            state_of(c * CHUNK + j)
        slab_copy(c).start()
        return carry

    def state_kept(i, carry):
        for j in range(CHUNK):
            state_of((mine + i) * CHUNK + j)
        return carry

    lax.fori_loop(0, near, state_sent, 0)
    lax.fori_loop(0, near, state_kept, 0)

    arrived(1)
    start(relay_up)
    start(relay_even)
    start(relay_odd)

    for b in range(2):
        aff[b] = dot_t(c_ref[half[b], :], b_ref[half[b], :])
    causal = lax.broadcasted_iota(jnp.int32, (BLOCK, BLOCK), 1) <= lax.broadcasted_iota(
        jnp.int32, (BLOCK, BLOCK), 0
    )

    def within_of(h):
        for b in range(2):
            spread = colb[h, half[b], :] - run[h, :, half[b]]
            weight = jnp.exp(jnp.where(causal, spread, FAR))
            mixing = (weight * aff[b]).astype(jnp.bfloat16)
            wbuf[half[b], lanes(h)] = dot(mixing, x_ref[half[b], lanes(h)])

    def relay(c):
        slab_copy(c).wait_recv()

        @pl.when(has_prev)
        def _():
            chain_copy(c).wait_recv()

        @pl.when(is_odd)
        def _():
            @pl.when(has_prev)
            def _():
                side_copy(c, ent).start()

            for i in range(CHUNK):
                h = c * CHUNK + i
                own = gpart[h] * ent[h].astype(jnp.float32) + partner_s[h].astype(jnp.float32)
                ent_own[h] = own.astype(jnp.bfloat16)
                eout[h] = (gdec[h] * own + slab[h].astype(jnp.float32)).astype(jnp.bfloat16)

        @pl.when(is_even)
        def _():
            for i in range(CHUNK):
                h = c * CHUNK + i
                ent_own[h] = ent[h]
                after = gdec[h] * ent[h].astype(jnp.float32) + slab[h].astype(jnp.float32)
                eside[h] = after.astype(jnp.bfloat16)
                eout[h] = (gpart[h] * after + partner_s[h].astype(jnp.float32)).astype(
                    jnp.bfloat16
                )
            side_copy(c, eside).start()

        @pl.when(has_next)
        def _():
            chain_copy(c).start()

    offset = jnp.minimum(d // 2 * 2 + 1, near)

    def relay_at(step):
        c = step - offset

        @pl.when((c >= 0) & (c < near))
        def _():
            relay(mine + c)

    decay_copy().wait_recv()

    per_within = heads // near

    def within_step(i, carry):
        for j in range(per_within):
            within_of(i * per_within + j)
        relay_at(i)
        return carry

    lax.fori_loop(0, near, within_step, 0)

    def label(positions):
        found = jnp.zeros(positions.shape, jnp.int32)
        for e in ends:
            found = found + jnp.where(positions >= e * BLOCK, 1, 0)
        return jnp.where(positions < 0, -1, found)

    q_pos = d * rows + lax.broadcasted_iota(jnp.int32, (rows, 1), 0)
    q_label = label(q_pos)
    for slot in range(CYCLE + 1):
        k_pos = (d - slot) * rows + lax.broadcasted_iota(jnp.int32, (1, rows), 1)
        same = (q_label == label(k_pos)) & (k_pos <= q_pos)
        bias[slot] = jnp.where(same, 0.0, FAR)

    factor = math.log2(math.e) / math.sqrt(WIDTH)
    per = q_heads // near

    def partial_of(h, slots):
        kh = h // group
        query = q_ref[:, lanes(h)]
        scores = []
        for slot in slots:
            key = k_ref[:, lanes(kh)] if slot == 0 else kv[slot - 1, 0, :, lanes(kh)]
            scores.append(dot_t(query, key) + bias[slot])
        top = scores[0]
        for s in scores[1:]:
            top = jnp.maximum(top, s)
        top = jnp.max(top, axis=1, keepdims=True)
        return scores, top

    def weigh(h, slots, scores, top):
        kh = h // group
        total = jnp.zeros((rows, rows), jnp.float32)
        result = jnp.zeros((rows, WIDTH), jnp.float32)
        for slot, s in zip(slots, scores):
            value = v_ref[:, lanes(kh)] if slot == 0 else kv[slot - 1, 1, :, lanes(kh)]
            weight = jnp.exp2((s - top) * factor)
            total = total + weight
            result = result + dot(weight.astype(jnp.bfloat16), value)
        return jnp.sum(total, axis=1, keepdims=True), result

    first = (0, 2, 4)
    second = (1, 3)

    def attend_first(h):
        scores, top = partial_of(h, first)
        total, result = weigh(h, first, scores, top)
        tops[h] = jnp.broadcast_to(top, (rows, WIDTH))
        sums_of[h] = jnp.broadcast_to(total, (rows, WIDTH))
        acc[h] = result

    def attend_second(h):
        scores, top = partial_of(h, second)
        before = tops[h]
        top = jnp.maximum(jnp.broadcast_to(top, (rows, WIDTH)), before)
        shrink = jnp.exp2((before - top) * factor)
        total, result = weigh(h, second, scores, top[:, :1])
        total = sums_of[h] * shrink + total
        att_ref[:, lanes(h)] = ((acc[h] * shrink + result) / total).astype(jnp.bfloat16)

    def first_step(i, carry):
        for j in range(per):
            attend_first(i * per + j)
        relay_at(near + i)
        return carry

    def second_step(i, carry):
        for j in range(per):
            attend_second(i * per + j)
        return carry

    arrived(3)
    start(last_odd)
    lax.fori_loop(0, near, first_step, 0)
    arrived(0)
    arrived(2)
    lax.fori_loop(0, near, second_step, 0)

    sq[...] = jnp.zeros(sq.shape, jnp.float32)

    def finish_of(h):
        entering = ent_own[h].astype(jnp.float32)
        g_0 = open_0 * jnp.exp(colb[h, BLOCK - 1 : BLOCK, :])
        later = g_0 * entering + s0[h].astype(jnp.float32)
        states = (ent_own[h], later.astype(jnp.bfloat16))
        for b in range(2):
            from_state = dot(c_ref[half[b], :], states[b])
            entry = opens[b] * jnp.exp(colb[h, half[b], :])
            mixed = wbuf[half[b], lanes(h)] + from_state * entry
            gate = g_ref[half[b], lanes(h)].astype(jnp.float32)
            gated = mixed * (gate / (1.0 + jnp.exp(-gate)))
            wbuf[half[b], lanes(h)] = gated
            sq[half[b], :] = sq[half[b], :] + gated * gated

    def finish_mine(i, carry):
        for j in range(CHUNK):
            finish_of((mine + i) * CHUNK + j)
        return carry

    def finish_theirs(i, carry):
        c = theirs + i

        @pl.when(is_odd | has_prev)
        def _():
            side_copy(c, ent).wait_recv()

        for j in range(CHUNK):
            finish_of(c * CHUNK + j)
        return carry

    lax.fori_loop(0, near, finish_mine, 0)
    lax.fori_loop(0, near, finish_theirs, 0)

    ss[...] = dot_t(jnp.ones((8, WIDTH), jnp.float32), sq[...], HIGH)

    def squares_copy(r):
        return pltpu.make_async_remote_copy(
            src_ref=ss, dst_ref=ssbuf.at[r - 1], send_sem=ss_send.at[r - 1],
            recv_sem=ss_recv.at[r - 1], device_id={"tp": lax.rem(t + r, n_tp)},
            device_id_type=MESH,
        )

    for r in range(1, n_tp):
        squares_copy(r).start()
    squares = ss[...]
    for r in range(1, n_tp):
        squares_copy(r).wait_recv()
        squares = squares + ssbuf[r - 1]
    spread_out = lax.dot_general(
        squares, jnp.full((8, WIDTH), 0.125, jnp.float32), (((0,), (0,)), ((), ())),
        preferred_element_type=jnp.float32, precision=HIGH,
    )
    sq[...] = lax.rsqrt(spread_out / features + 1e-05)

    def scale_out(h, carry):
        out_ref[:, lanes(h)] = (
            wbuf[:, lanes(h)] * sq[...] * gain_ref[:, lanes(h)]
        ).astype(jnp.bfloat16)
        return carry

    lax.fori_loop(0, heads, scale_out, 0)

    for r in range(1, n_tp):
        squares_copy(r).wait_send()
    for move in (own_up, own_side, relay_up, relay_even, relay_odd, last_odd):
        sent(move)

    decay_copy().wait_send()

    def drain(i, carry):
        slab_copy(theirs + i).wait_send()

        @pl.when(is_even | has_prev)
        def _():
            side_copy(mine + i, ent).wait_send()

        @pl.when(has_next)
        def _():
            chain_copy(mine + i).wait_send()

        return carry

    lax.fori_loop(0, near, drain, 0)


def on_device(n_seq, n_tp, *args):
    (x, gate, write, read, decay, gain, q, k, v, request_blocks) = args
    rows = x.shape[0]
    heads = decay.shape[0]
    chunks = heads // CHUNK
    f32, bf16 = jnp.float32, jnp.bfloat16
    states = pltpu.VMEM((heads, WIDTH, WIDTH), bf16)
    softmax = pltpu.VMEM((q.shape[1] // WIDTH, rows, WIDTH), f32)
    dma = pltpu.SemaphoreType.DMA
    vmem = pl.BlockSpec(memory_space=pltpu.VMEM)
    return pl.pallas_call(
        partial(kernel, n_seq, n_tp, heads * n_tp * WIDTH),
        out_shape=(
            jax.ShapeDtypeStruct(x.shape, bf16),
            jax.ShapeDtypeStruct(q.shape, bf16),
        ),
        in_specs=[pl.BlockSpec(memory_space=pltpu.SMEM)] + [vmem] * 9,
        out_specs=(vmem, vmem),
        scratch_shapes=[
            pltpu.VMEM((CYCLE, 2) + k.shape, bf16),
            pltpu.VMEM((CYCLE + 1, rows, rows), f32),
            pltpu.VMEM((heads, 1, rows), f32),
            pltpu.VMEM((heads, rows, WIDTH), f32),
            pltpu.VMEM((WIDTH, rows), bf16),
            pltpu.VMEM((2, BLOCK, BLOCK), f32),
            pltpu.VMEM(x.shape, f32),
            states, states, states, states, states, states, states,
            softmax, softmax, softmax,
            pltpu.VMEM((heads, 1, WIDTH), f32),
            pltpu.VMEM((heads, 1, WIDTH), f32),
            pltpu.VMEM((rows, WIDTH), f32),
            pltpu.VMEM((8, rows), f32),
            pltpu.VMEM((n_tp - 1, 8, rows), f32),
            dma((5, 2)), dma((CYCLE, 2)),
            dma((chunks,)), dma((chunks,)), dma((chunks,)), dma((chunks,)), dma((chunks,)),
            dma((chunks,)),
            dma((2,)), dma((n_tp - 1,)), dma((n_tp - 1,)),
        ],
        compiler_params=pltpu.CompilerParams(
            collective_id=0, has_side_effects=True, vmem_limit_bytes=60 * 1024 * 1024
        ),
    )(request_blocks, x, gate, write, read, decay, gain.reshape(1, -1), q, k, v)


def solution(mesh):
    placed = (
        P("seq", "tp"),
        P("seq", "tp"),
        P("seq", None),
        P("seq", None),
        P("tp", "seq"),
        P("tp"),
        P("seq", "tp"),
        P("seq", "tp"),
        P("seq", "tp"),
        P(),
    )
    return jax.shard_map(
        partial(on_device, mesh.shape["seq"], mesh.shape["tp"]),
        mesh=mesh,
        in_specs=placed,
        out_specs=(P("seq", "tp"), P("seq", "tp")),
        check_vma=False,
    )
```

```python
from functools import partial
import math

import jax
import jax.numpy as jnp
from jax import lax
from jax.experimental import pallas as pl
from jax.experimental.pallas import tpu as pltpu
from jax.sharding import PartitionSpec as P

WIDTH = 128
BLOCK = 128
CYCLE = 4
CHUNK = 2
FAR = -1e30
MESH = pl.DeviceIdType.MESH
HIGH = lax.Precision.HIGHEST


def lanes(h):
    return pl.ds(pl.multiple_of(h * WIDTH, WIDTH), WIDTH)


def dot_t(a, b, precision=None):
    return lax.dot_general(
        a, b, (((1,), (1,)), ((), ())), preferred_element_type=jnp.float32, precision=precision
    )


def dot(a, b, precision=None):
    return jnp.dot(a, b, preferred_element_type=jnp.float32, precision=precision)


def kernel(
    n_seq, n_tp, features,
    rb, x_ref, g_ref, b_ref, c_ref, ld_ref, q_ref, k_ref, v_ref,
    wbuf, att_ref, scale_ref,
    kv, bias, run, colb, bt, aff, s0, slab, partner_s, ent, ent_own, eout, eside,
    acc, tops, masks, q_vm, g_vm, gdec, gpart, sq, ss, ssbuf,
    load_sem, kv_send, kv_recv, st_send, st_recv, ev_send, e_recv, ch_send, c_recv, gd_sem, ss_send, ss_recv,
):
    d = lax.axis_index("seq")
    t = lax.axis_index("tp")
    odd = lax.rem(d, 2)
    is_odd = odd == 1
    is_even = odd == 0
    partner = d + 1 - 2 * odd
    has_next = d + 2 < n_seq
    has_prev = d >= 2
    rows = x_ref.shape[0]
    heads = ld_ref.shape[0]
    q_heads = q_ref.shape[1] // WIDTH
    kv_heads = k_ref.shape[1] // WIDTH
    group = q_heads // kv_heads
    near = heads // CHUNK // 2
    mine = odd * near
    theirs = near - mine
    half = (slice(0, BLOCK), slice(BLOCK, 2 * BLOCK))

    q_load = pltpu.make_async_copy(q_ref, q_vm, load_sem.at[0])
    g_load = pltpu.make_async_copy(g_ref, g_vm, load_sem.at[1])
    q_load.start()
    g_load.start()

    barrier = pltpu.get_barrier_semaphore()
    pl.semaphore_signal(barrier, inc=1, device_id={"seq": partner}, device_id_type=MESH)
    for r in range(1, n_tp):
        pl.semaphore_signal(
            barrier, inc=1, device_id={"tp": lax.rem(t + r, n_tp)}, device_id_type=MESH
        )

    @pl.when(has_next)
    def _():
        pl.semaphore_signal(barrier, inc=1, device_id={"seq": d + 2}, device_id_type=MESH)

    @pl.when(has_prev)
    def _():
        pl.semaphore_signal(barrier, inc=1, device_id={"seq": d - 2}, device_id_type=MESH)

    peers = n_tp + has_next.astype(jnp.int32) + has_prev.astype(jnp.int32)
    pl.semaphore_wait(barrier, peers)

    def kv_copy(part, source, send, slot, target):
        own = (k_ref, v_ref)[part]
        return pltpu.make_async_remote_copy(
            src_ref=own if source is None else kv.at[source, part],
            dst_ref=kv.at[slot, part],
            send_sem=kv_send.at[send, part],
            recv_sem=kv_recv.at[slot, part],
            device_id={"seq": target},
            device_id_type=MESH,
        )

    own_up = (has_next, None, 0, 1, d + 2)
    own_side = (is_even, None, 1, 0, d + 1)
    relay_up = (has_prev & has_next, 1, 2, 3, d + 2)
    relay_even = (has_prev & is_even, 1, 1 + 2, 2, d + 1)
    relay_odd = (has_prev & is_odd, 1, 1 + 2, 0, d - 1)
    last_odd = ((d >= 4) & is_odd, 3, 4, 2, d - 1)

    def start(move):
        @pl.when(move[0])
        def _():
            for part in range(2):
                kv_copy(part, *move[1:]).start()

    def sent(move):
        @pl.when(move[0])
        def _():
            for part in range(2):
                kv_copy(part, *move[1:]).wait_send()

    def arrived(slot):
        @pl.when(d >= slot + 1)
        def _():
            for part in range(2):
                kv_copy(part, None, 0, slot, partner).wait_recv()

    start(own_up)
    start(own_side)
    for slot in range(CYCLE):
        @pl.when(d < slot + 1)
        def _():
            kv[slot] = jnp.zeros(kv.shape[1:], kv.dtype)

    span = near * CHUNK

    @pl.when(d < 2)
    def _():
        ent[pl.ds(mine * CHUNK, span)] = jnp.zeros((span,) + ent.shape[1:], ent.dtype)

    @pl.when((d < 2) & is_even)
    def _():
        ent_own[pl.ds(theirs * CHUNK, span)] = jnp.zeros((span,) + ent.shape[1:], ent.dtype)

    ends = []
    total = jnp.int32(0)
    for i in range(4):
        total = total + rb[i]
        ends.append(total)

    def opened(block):
        flag = jnp.where(block == 0, 0.0, 1.0)
        for e in ends:
            flag = flag * jnp.where(block == e, 0.0, 1.0)
        return flag

    open_0 = opened(2 * d)
    open_1 = opened(2 * d + 1)
    opens = (open_0, open_1)

    i_r = lax.broadcasted_iota(jnp.int32, (rows, rows), 0)
    i_c = lax.broadcasted_iota(jnp.int32, (rows, rows), 1)
    lower = jnp.where((i_c <= i_r) & (i_r // BLOCK == i_c // BLOCK), 1.0, 0.0)
    decays = ld_ref[...]
    sums_row = dot_t(decays, lower, HIGH)
    columns = dot_t(lower, decays, HIGH)
    for h in range(heads):
        colb[h] = jnp.broadcast_to(columns[:, h : h + 1], (rows, WIDTH))
        run[h] = sums_row[h : h + 1, :]
        gdec[h] = open_0 * open_1 * jnp.exp(
            colb[h, BLOCK - 1 : BLOCK, :] + colb[h, 2 * BLOCK - 1 : 2 * BLOCK, :]
        )

    def decay_copy():
        return pltpu.make_async_remote_copy(
            src_ref=gdec, dst_ref=gpart, send_sem=gd_sem.at[0], recv_sem=gd_sem.at[1],
            device_id={"seq": partner}, device_id_type=MESH,
        )

    decay_copy().start()
    bt[...] = b_ref[...].astype(jnp.float32).T.astype(jnp.bfloat16)

    def part_of(ref, c):
        return ref.at[pl.ds(c * CHUNK, CHUNK)]

    def slab_copy(c):
        return pltpu.make_async_remote_copy(
            src_ref=part_of(slab, c), dst_ref=part_of(partner_s, c),
            send_sem=st_send.at[c], recv_sem=st_recv.at[c],
            device_id={"seq": partner}, device_id_type=MESH,
        )

    def side_copy(c, source):
        return pltpu.make_async_remote_copy(
            src_ref=part_of(source, c), dst_ref=part_of(ent_own, c),
            send_sem=ev_send.at[c], recv_sem=e_recv.at[c],
            device_id={"seq": partner}, device_id_type=MESH,
        )

    def chain_copy(c):
        return pltpu.make_async_remote_copy(
            src_ref=part_of(eout, c), dst_ref=part_of(ent, c),
            send_sem=ch_send.at[c], recv_sem=c_recv.at[c],
            device_id={"seq": d + 2}, device_id_type=MESH,
        )

    def state_of(h):
        states = []
        for b in range(2):
            last_row = colb[h, b * BLOCK + BLOCK - 1 : b * BLOCK + BLOCK, :]
            reach = jnp.exp(last_row - colb[h, half[b], :])
            carried = (x_ref[half[b], lanes(h)].astype(jnp.float32) * reach).astype(jnp.bfloat16)
            states.append(dot(bt[:, half[b]], carried))
        g_1 = open_1 * jnp.exp(colb[h, 2 * BLOCK - 1 : 2 * BLOCK, :])
        s0[h] = states[0].astype(jnp.bfloat16)
        slab[h] = (g_1 * states[0] + states[1]).astype(jnp.bfloat16)

    def state_sent(i, carry):
        c = theirs + i
        for j in range(CHUNK):
            state_of(c * CHUNK + j)
        slab_copy(c).start()
        return carry

    def state_kept(i, carry):
        for j in range(CHUNK):
            state_of((mine + i) * CHUNK + j)
        return carry

    lax.fori_loop(0, near, state_sent, 0)
    lax.fori_loop(0, near, state_kept, 0)

    arrived(1)
    start(relay_up)
    start(relay_even)
    start(relay_odd)

    for b in range(2):
        aff[b] = dot_t(c_ref[half[b], :], b_ref[half[b], :])
    causal = lax.broadcasted_iota(jnp.int32, (BLOCK, BLOCK), 1) <= lax.broadcasted_iota(
        jnp.int32, (BLOCK, BLOCK), 0
    )

    def within_of(h):
        for b in range(2):
            spread = colb[h, half[b], :] - run[h, :, half[b]]
            weight = jnp.exp(jnp.where(causal, spread, FAR))
            mixing = (weight * aff[b]).astype(jnp.bfloat16)
            wbuf[half[b], lanes(h)] = dot(mixing, x_ref[half[b], lanes(h)])

    def relay(c):
        slab_copy(c).wait_recv()

        @pl.when(has_prev)
        def _():
            chain_copy(c).wait_recv()

        @pl.when(is_odd)
        def _():
            @pl.when(has_prev)
            def _():
                side_copy(c, ent).start()

            for i in range(CHUNK):
                h = c * CHUNK + i
                own = gpart[h] * ent[h].astype(jnp.float32) + partner_s[h].astype(jnp.float32)
                ent_own[h] = own.astype(jnp.bfloat16)
                eout[h] = (gdec[h] * own + slab[h].astype(jnp.float32)).astype(jnp.bfloat16)

        @pl.when(is_even)
        def _():
            for i in range(CHUNK):
                h = c * CHUNK + i
                ent_own[h] = ent[h]
                after = gdec[h] * ent[h].astype(jnp.float32) + slab[h].astype(jnp.float32)
                eside[h] = after.astype(jnp.bfloat16)
                eout[h] = (gpart[h] * after + partner_s[h].astype(jnp.float32)).astype(
                    jnp.bfloat16
                )
            side_copy(c, eside).start()

        @pl.when(has_next)
        def _():
            chain_copy(c).start()

    offset = jnp.minimum(d // 2 * 2 + 1, near)

    def relay_at(step):
        c = step - offset

        @pl.when((c >= 0) & (c < near))
        def _():
            relay(mine + c)

    decay_copy().wait_recv()

    per_within = heads // near

    def within_step(i, carry):
        for j in range(per_within):
            within_of(i * per_within + j)
        relay_at(i)
        return carry

    lax.fori_loop(0, near, within_step, 0)

    def label(positions):
        found = jnp.zeros(positions.shape, jnp.int32)
        for e in ends:
            found = found + jnp.where(positions >= e * BLOCK, 1, 0)
        return jnp.where(positions < 0, -1, found)

    q_pos = d * rows + lax.broadcasted_iota(jnp.int32, (rows, 1), 0)
    own_pos = d * rows + lax.broadcasted_iota(jnp.int32, (1, rows), 1)
    bias[...] = jnp.where((label(q_pos) == label(own_pos)) & (own_pos <= q_pos), 0.0, FAR)
    line = lax.broadcasted_iota(jnp.int32, (rows, WIDTH), 0)
    lane = lax.broadcasted_iota(jnp.int32, (rows, WIDTH), 1)
    lane_label = label(d * rows + jnp.minimum(lane, 1) * BLOCK)
    select = jnp.where(lane == line // BLOCK, 1.0, 0.0).astype(jnp.bfloat16)
    ones = jnp.ones((rows, WIDTH), jnp.bfloat16)
    for slot in range(1, CYCLE + 1):
        other = label((d - slot) * rows + line) != lane_label
        masks[slot - 1] = jnp.where(other & (lane < 2), FAR, 0.0).astype(jnp.bfloat16)

    q_load.wait()
    factor = math.log2(math.e) / math.sqrt(WIDTH)
    per = q_heads // near

    def twice(a):
        return jnp.concatenate([a, a], axis=1)

    def scores_of(h, slots):
        kh = h // group
        query = q_vm[:, lanes(h)]
        wide = jnp.concatenate([query, select], axis=1)
        scores = []
        for slot in slots:
            if slot == 0:
                scores.append(dot_t(query, k_ref[:, lanes(kh)]) + bias[...])
            else:
                key = jnp.concatenate([kv[slot - 1, 0, :, lanes(kh)], masks[slot - 1]], axis=1)
                scores.append(dot_t(wide, key))
        top = scores[0]
        for s in scores[1:]:
            top = jnp.maximum(top, s)
        top = jnp.max(top, axis=1, keepdims=True)
        return scores, jnp.broadcast_to(top, (rows, WIDTH))

    def weigh(h, slots, scores, top):
        kh = h // group
        result = None
        for slot, s in zip(slots, scores):
            value = v_ref[:, lanes(kh)] if slot == 0 else kv[slot - 1, 1, :, lanes(kh)]
            weight = jnp.exp2((s - twice(top)) * factor).astype(jnp.bfloat16)
            part = dot(weight, jnp.concatenate([value, ones], axis=1))
            result = part if result is None else result + part
        return result

    first = (0, 2, 4)
    second = (1, 3)

    def attend_first(h):
        scores, top = scores_of(h, first)
        tops[h] = top
        acc[h] = weigh(h, first, scores, top)

    def attend_second(h):
        scores, top = scores_of(h, second)
        before = tops[h]
        top = jnp.maximum(top, before)
        shrink = jnp.exp2((before - top) * factor)
        result = acc[h] * twice(shrink) + weigh(h, second, scores, top)
        att_ref[:, lanes(h)] = (result[:, :WIDTH] / result[:, WIDTH:]).astype(jnp.bfloat16)

    def first_step(i, carry):
        for j in range(per):
            attend_first(i * per + j)
        relay_at(near + i)
        return carry

    def second_step(i, carry):
        for j in range(per):
            attend_second(i * per + j)
        return carry

    arrived(3)
    start(last_odd)
    lax.fori_loop(0, near, first_step, 0)
    arrived(0)
    arrived(2)
    lax.fori_loop(0, near, second_step, 0)

    sq[...] = jnp.zeros(sq.shape, jnp.float32)

    def finish_of(h):
        entering = ent_own[h].astype(jnp.float32)
        g_0 = open_0 * jnp.exp(colb[h, BLOCK - 1 : BLOCK, :])
        later = g_0 * entering + s0[h].astype(jnp.float32)
        states = (ent_own[h], later.astype(jnp.bfloat16))
        for b in range(2):
            from_state = dot(c_ref[half[b], :], states[b])
            entry = opens[b] * jnp.exp(colb[h, half[b], :])
            mixed = wbuf[half[b], lanes(h)] + from_state * entry
            gate = 0.5 * g_vm[half[b], lanes(h)].astype(jnp.float32)
            gated = mixed * (gate + gate * jnp.tanh(gate))
            wbuf[half[b], lanes(h)] = gated
            sq[half[b], :] = sq[half[b], :] + gated * gated

    def finish_mine(i, carry):
        for j in range(CHUNK):
            finish_of((mine + i) * CHUNK + j)
        return carry

    def finish_theirs(i, carry):
        c = theirs + i

        @pl.when(is_odd | has_prev)
        def _():
            side_copy(c, ent).wait_recv()

        for j in range(CHUNK):
            finish_of(c * CHUNK + j)
        return carry

    g_load.wait()
    lax.fori_loop(0, near, finish_mine, 0)
    lax.fori_loop(0, near, finish_theirs, 0)

    ss[...] = dot_t(jnp.ones((8, WIDTH), jnp.float32), sq[...], HIGH)

    def squares_copy(r):
        return pltpu.make_async_remote_copy(
            src_ref=ss, dst_ref=ssbuf.at[r - 1], send_sem=ss_send.at[r - 1],
            recv_sem=ss_recv.at[r - 1], device_id={"tp": lax.rem(t + r, n_tp)},
            device_id_type=MESH,
        )

    for r in range(1, n_tp):
        squares_copy(r).start()
    squares = ss[...]
    for r in range(1, n_tp):
        squares_copy(r).wait_recv()
        squares = squares + ssbuf[r - 1]
    spread_out = lax.dot_general(
        squares, jnp.full((8, WIDTH), 0.125, jnp.float32), (((0,), (0,)), ((), ())),
        preferred_element_type=jnp.float32, precision=HIGH,
    )
    scale_ref[...] = lax.rsqrt(spread_out / features + 1e-05)

    for r in range(1, n_tp):
        squares_copy(r).wait_send()
    for move in (own_up, own_side, relay_up, relay_even, relay_odd, last_odd):
        sent(move)

    decay_copy().wait_send()

    def drain(i, carry):
        slab_copy(theirs + i).wait_send()

        @pl.when(is_even | has_prev)
        def _():
            side_copy(mine + i, ent).wait_send()

        @pl.when(has_next)
        def _():
            chain_copy(mine + i).wait_send()

        return carry

    lax.fori_loop(0, near, drain, 0)


def on_device(n_seq, n_tp, *args):
    (x, gate, write, read, decay, gain, q, k, v, request_blocks) = args
    rows = x.shape[0]
    heads = decay.shape[0]
    chunks = heads // CHUNK
    f32, bf16 = jnp.float32, jnp.bfloat16
    states = pltpu.VMEM((heads, WIDTH, WIDTH), bf16)
    softmax = pltpu.VMEM((q.shape[1] // WIDTH, rows, WIDTH), f32)
    dma = pltpu.SemaphoreType.DMA
    vmem = pl.BlockSpec(memory_space=pltpu.VMEM)
    hbm = pl.BlockSpec(memory_space=pl.ANY)
    gated, attention, scale = pl.pallas_call(
        partial(kernel, n_seq, n_tp, heads * n_tp * WIDTH),
        out_shape=(
            jax.ShapeDtypeStruct(x.shape, f32),
            jax.ShapeDtypeStruct(q.shape, bf16),
            jax.ShapeDtypeStruct((rows, WIDTH), f32),
        ),
        in_specs=[pl.BlockSpec(memory_space=pltpu.SMEM), vmem, hbm, vmem, vmem, vmem, hbm, vmem, vmem],
        out_specs=(vmem, vmem, vmem),
        scratch_shapes=[
            pltpu.VMEM((CYCLE, 2) + k.shape, bf16),
            pltpu.VMEM((rows, rows), f32),
            pltpu.VMEM((heads, 1, rows), f32),
            pltpu.VMEM((heads, rows, WIDTH), f32),
            pltpu.VMEM((WIDTH, rows), bf16),
            pltpu.VMEM((2, BLOCK, BLOCK), f32),
            states, states, states, states, states, states, states,
            pltpu.VMEM((q.shape[1] // WIDTH, rows, 2 * WIDTH), f32), softmax,
            pltpu.VMEM((CYCLE, rows, WIDTH), bf16), pltpu.VMEM(q.shape, bf16), pltpu.VMEM(x.shape, bf16),
            pltpu.VMEM((heads, 1, WIDTH), f32),
            pltpu.VMEM((heads, 1, WIDTH), f32),
            pltpu.VMEM((rows, WIDTH), f32),
            pltpu.VMEM((8, rows), f32),
            pltpu.VMEM((n_tp - 1, 8, rows), f32),
            dma((2,)), dma((5, 2)), dma((CYCLE, 2)),
            dma((chunks,)), dma((chunks,)), dma((chunks,)), dma((chunks,)), dma((chunks,)),
            dma((chunks,)),
            dma((2,)), dma((n_tp - 1,)), dma((n_tp - 1,)),
        ],
        compiler_params=pltpu.CompilerParams(
            collective_id=0, has_side_effects=True, vmem_limit_bytes=60 * 1024 * 1024
        ),
    )(request_blocks, x, gate, write, read, decay, q, k, v)
    out = gated * scale[:, :1] * gain[None, :]
    return out.astype(bf16), attention


def solution(mesh):
    placed = (
        P("seq", "tp"),
        P("seq", "tp"),
        P("seq", None),
        P("seq", None),
        P("tp", "seq"),
        P("tp"),
        P("seq", "tp"),
        P("seq", "tp"),
        P("seq", "tp"),
        P(),
    )
    return jax.shard_map(
        partial(on_device, mesh.shape["seq"], mesh.shape["tp"]),
        mesh=mesh,
        in_specs=placed,
        out_specs=(P("seq", "tp"), P("seq", "tp")),
        check_vma=False,
    )
```
